32 devices in a mesh: groups: 2 (over y), ep: 4 (over z), tp: 4 (over x, core).
Axes of the slice: x: 2, y: 2, z: 4, core: 2. Of those that a mesh axis runs over, the one named last changes fastest.
Arguments:
- tokens: bfloat16 [2, 512, 4096], P(None, ('groups', 'ep')), parts along dimension 1, may hold values from -6 to 6
- expert_ids: int32 [2, 512, 2], P(None, ('groups', 'ep')), parts along dimension 1, may hold values from 0 to 1, all different within a row
- gate_weights: float32 [2, 512, 2], P(None, ('groups', 'ep')), parts along dimension 1, may hold values from 0.05 to 1
- replica_pick: int32 [2, 512, 2], P(None, ('groups', 'ep')), parts along dimension 1, may hold values from 0 to 3
- placement: int32 [2, 4], replicated, may hold values from 0 to 1, as said below
- slot_limit: int32 [4], replicated, may hold values from 20 to 40, as said below
- expert_weights: bfloat16 [4, 3, 1536, 4096], P('ep', None, 'tp'), as said below
Outputs:
- layer_out: bfloat16 [2, 512, 4096], P(None, ('groups', 'ep'), 'tp'), parts along dimension 1
The draws below stay inside these ranges and needn't reach their ends.
There are 2 independent parts, one for each index of `groups`. The reference program is written for one: setup_inputs(seed, part) draws one part's arguments, and reference() takes and returns one part's arrays. A program takes and returns all parts, laid end to end along the dimension named above; an argument that names none is the same for every part. Nothing has to cross between parts.
Inputs may be any that keep to these rules, and one draw needn't show every extreme that they name: `expert_ids`: each row names 2 different experts, and every expert is named somewhere. `placement`: row 0 is the old and row 1 the new slot-to-expert table. In each table every expert is held by one or more slots, and exactly 2 slots hold another expert in row 1 than in row 0. `slot_limit`: some slot has capacity exactly 40. `expert_weights`: slots that hold the same expert in the old table hold equal weights.
All inputs are finite; a program needn't handle non-finite values.
Results may differ from the reference program's by a relative error of at most 0.015.
Values may be sent and summed in bfloat16 or wider, within the bound.
A program may use at most 128 MiB of HBM per device.

```python
import math
import jax
import jax.numpy as jnp
from jax import lax

D = 4096
FF = 1536
TOK_DEV = 64
SLOTS = 4
REDUND = 2
EXPERTS = 2
TOP = 2
CAP = 40
TOKENS = 256
N_EP = 4
N_TP = 4


def tables(table_key):
    key_first, key_second, key_third = jax.random.split(table_key, 3)
    base_slot = jax.random.randint(key_first, (), 0, SLOTS).astype(jnp.int32)
    expert_order = jax.random.permutation(key_second, EXPERTS).astype(jnp.int32)
    position = jnp.arange(EXPERTS, dtype=jnp.int32)
    primary_slots = ((base_slot + REDUND + position) % SLOTS).astype(jnp.int32)
    old_table = jnp.zeros((SLOTS,), jnp.int32).at[primary_slots].set(expert_order)
    far_position = SLOTS // 2 + 1 - REDUND
    near_position = EXPERTS - 1
    if far_position == near_position:
        free_count = EXPERTS - 1
    else:
        free_count = EXPERTS - 2
    free_draw = jax.random.randint(key_third, (REDUND,), 0, free_count).astype(jnp.int32)
    free_position = jnp.where(free_draw >= far_position, free_draw + 1, free_draw).astype(jnp.int32)
    old_extra = expert_order[free_position]
    source_position = jnp.full((REDUND,), near_position, jnp.int32).at[1].set(far_position)
    new_extra = expert_order[source_position]
    target_slots = ((base_slot + jnp.arange(REDUND, dtype=jnp.int32)) % SLOTS).astype(jnp.int32)
    new_table = old_table.at[target_slots].set(new_extra)
    old_table = old_table.at[target_slots].set(old_extra)
    return (old_table, new_table)


def draw_placement(key, part):
    old_table, new_table = tables(jax.random.fold_in(key, 11))
    return jnp.stack([old_table, new_table]).astype(jnp.int32)


def draw_expert_weights(key, part):
    old_table, new_table = tables(jax.random.fold_in(key, 11))
    normal_draw = jax.random.normal(jax.random.fold_in(key, 12), (EXPERTS, 3, FF, D), jnp.float32)
    scales = jnp.array([D ** (-0.5), D ** (-0.5), FF ** (-0.5)], jnp.float32)
    scaled = normal_draw * scales[None, :, None, None]
    return scaled[old_table].astype(jnp.bfloat16)


def draw_slot_limit(key, part):
    inner_key = jax.random.fold_in(key, 13)
    limits = jax.random.randint(inner_key, (SLOTS,), CAP // 2, CAP + 1)
    filled = jax.random.randint(jax.random.fold_in(inner_key, 1), (), 0, SLOTS)
    return jnp.where(jnp.arange(SLOTS) == filled, CAP, limits).astype(jnp.int32)


def plant(entries, own_key, smallest, largest):
    longest = entries.shape.index(max(entries.shape))
    spots = []
    for shift in (0, 1):
        where = [jax.random.randint(jax.random.fold_in(own_key, axis), (), 0, length) for axis, length in enumerate(entries.shape)]
        where[longest] = (where[longest] + shift) % entries.shape[longest]
        spots.append(tuple(where))
    return entries.at[spots[0]].set(smallest).at[spots[1]].set(largest)


def level_of(key, dims, shards, smallest, largest):
    loudness = 1.0
    for axis_at, shards_of in shards:
        steps = jax.random.uniform(jax.random.fold_in(jax.random.fold_in(key, 6), axis_at), (shards_of,), jnp.float32, smallest / len(shards), largest / len(shards))
        loudness = loudness * jnp.repeat(jnp.exp(steps), dims[axis_at] // shards_of).reshape((-1,) + (1,) * (len(dims) - 1 - axis_at))
    return loudness


def choose_distinct(stream_key, rows, number_of, top, lift):
    sequence = jax.random.permutation(jax.random.fold_in(stream_key, 1), number_of)
    boost = sequence
    for power in range(3):
        boost = boost * boost // number_of
    boost = boost * lift // number_of
    tickets = jax.random.randint(jax.random.fold_in(stream_key, 2), (rows, number_of), 0, 4096) + boost
    fixed_rows = jax.random.permutation(jax.random.fold_in(stream_key, 3), rows)[jnp.arange(number_of) % rows]
    tickets = jnp.where(jnp.arange(rows)[:, None] == fixed_rows[None, :], 1 << 14, tickets)
    merit = tickets * number_of + jnp.arange(number_of)
    return lax.top_k(merit.astype(jnp.int32), top)[1].astype(jnp.int32)


def centred(rng, extent, scale, reach, cuts=(), kind=jnp.bfloat16):
    gain = level_of(rng, extent, cuts, -0.22, 0.18) if cuts else 1.0
    values = jax.random.normal(rng, extent, jnp.float32) * scale * gain
    return jnp.minimum(jnp.maximum(values, -reach), reach).astype(kind)


def setup_inputs(seed: int = 0, part: int = 0) -> dict:
    keys = jax.random.split(jax.random.key(seed), 8)
    part_splits = jax.random.split(jax.random.fold_in(keys[7], part), 8)
    tokens = centred(part_splits[0], (2, TOKENS, D), 1.0, 6.0, ((1, 4),))
    expert_ids = choose_distinct(part_splits[1], 2 * TOKENS, EXPERTS, TOP, 12000).reshape((2, TOKENS, TOP))
    gate_weights = jnp.clip(jnp.exp(math.log(1.0) - 2.9957323 * jax.random.uniform(part_splits[2], (2, TOKENS, TOP), jnp.float32) ** level_of(part_splits[2], (2, TOKENS, TOP), ((1, 4),), -0.2, 0.2)), 0.05, 1.0)
    replica_pick = plant(jax.random.randint(part_splits[3], (2, TOKENS, TOP), 0, 4), jax.random.fold_in(part_splits[3], 1), 0, 3).astype(jnp.int32)
    placement = draw_placement(jax.random.fold_in(keys[7], 71), part)
    slot_limit = draw_slot_limit(jax.random.fold_in(keys[7], 71), part)
    expert_weights = draw_expert_weights(jax.random.fold_in(keys[7], 71), part)
    return dict(tokens=tokens, expert_ids=expert_ids, gate_weights=gate_weights, replica_pick=replica_pick, placement=placement, slot_limit=slot_limit, expert_weights=expert_weights)


def slot_choice(slot_table, chosen_ids, pick_values, slot_count):
    slot_range = jnp.arange(slot_count, dtype=jnp.int32)
    holders = (slot_table[None, None, :] == chosen_ids[:, :, None]).astype(jnp.int32)
    holder_count = jnp.sum(holders, axis=2)
    earlier = jnp.cumsum(holders, axis=2) - holders
    wanted = pick_values % holder_count
    matched = holders * (earlier == wanted[:, :, None]).astype(jnp.int32)
    return jnp.sum(matched * slot_range[None, None, :], axis=2)


def placements(slot_table, limits, chosen_ids, pick_values, block_rows, capacity):
    slot_count = slot_table.shape[0]
    chosen = slot_choice(slot_table, chosen_ids, pick_values, slot_count)
    row_count, top_count = chosen.shape
    blocked = chosen.reshape(row_count // block_rows, block_rows * top_count)
    onehot = (blocked[:, :, None] == jnp.arange(slot_count, dtype=jnp.int32)[None, None, :]).astype(jnp.int32)
    ranked = jnp.sum(onehot * (jnp.cumsum(onehot, axis=1) - onehot), axis=2)
    allowed = jnp.sum(onehot * limits[None, None, :], axis=2)
    located = jnp.where(ranked < allowed, blocked * capacity + ranked, slot_count * capacity)
    return located.reshape(row_count, top_count)


def expert_apply(inputs, weights):
    gate_proj = jnp.dot(inputs, weights[0].T, preferred_element_type=jnp.float32)
    upward = jnp.dot(inputs, weights[1].T, preferred_element_type=jnp.float32)
    hidden = (jax.nn.silu(gate_proj) * upward).astype(jnp.bfloat16)
    group_size = hidden.shape[1] // N_TP
    summed = jnp.zeros((inputs.shape[0], inputs.shape[1]), jnp.float32)
    for member in range(N_TP):
        lower = member * group_size
        partial_out = jnp.dot(hidden[:, lower:lower + group_size], weights[2, lower:lower + group_size],
                              preferred_element_type=jnp.float32).astype(jnp.bfloat16)
        partial_out = lax.optimization_barrier(partial_out)
        summed = summed + partial_out.astype(jnp.float32)
    return summed.astype(jnp.bfloat16)


def run_span(span_rows, chosen_ids, weight_values, pick_values, slot_table, limits, weights):
    located = placements(slot_table, limits, chosen_ids, pick_values, TOK_DEV, CAP)
    token_index = jnp.arange(TOKENS, dtype=jnp.int32)
    source_block = token_index // TOK_DEV
    kept_mask = located < SLOTS * CAP
    slot_index = located // CAP
    rank_index = located % CAP
    buffer_index = jnp.where(kept_mask, slot_index * (N_EP * CAP) + source_block[:, None] * CAP + rank_index,
                             SLOTS * N_EP * CAP).astype(jnp.int32)
    token_source = jnp.full((SLOTS * N_EP * CAP + 1,), TOKENS, jnp.int32)
    spread = jnp.broadcast_to(token_index[:, None], buffer_index.shape).reshape(-1)
    token_source = token_source.at[buffer_index.reshape(-1)].set(spread)[:-1]
    padded_rows = jnp.concatenate([span_rows, jnp.zeros((1, D), jnp.bfloat16)])
    buffers = padded_rows[token_source].reshape(SLOTS, N_EP * CAP, D)
    outputs = lax.map(lambda operands: expert_apply(operands[0], operands[1]), (buffers, weights))
    flat_out = jnp.concatenate([outputs.reshape(SLOTS * N_EP * CAP, D), jnp.zeros((1, D), jnp.bfloat16)])
    combined = jnp.zeros((TOKENS, D), jnp.float32)
    for member in range(TOP):
        combined = combined + weight_values[:, member, None] * flat_out[buffer_index[:, member]].astype(jnp.float32)
    return combined.astype(jnp.bfloat16)


def reference(tokens, expert_ids, gate_weights, replica_pick, placement, slot_limit, expert_weights):
    first_out = run_span(tokens[0], expert_ids[0], gate_weights[0], replica_pick[0], placement[0],
                          slot_limit, expert_weights)
    slot_range = jnp.arange(SLOTS, dtype=jnp.int32)
    matches = placement[0][None, :] == placement[1][:, None]
    sources = jnp.min(jnp.where(matches, slot_range[None, :], SLOTS), axis=1).astype(jnp.int32)
    relocated = expert_weights[sources]
    second_out = run_span(tokens[1], expert_ids[1], gate_weights[1], replica_pick[1], placement[1],
                           slot_limit, relocated)
    return jnp.stack([first_out, second_out])
```

```python
import functools

import jax
import jax.numpy as jnp
from jax import lax
from jax.experimental import pallas as pl
from jax.experimental.pallas import tpu as pltpu
from jax.sharding import PartitionSpec as P

MESH = pl.DeviceIdType.MESH


def kernel(
    E, T, tokens, ids, gates, replica, table, limits, placement, weights, out,
    w, x, p, r1, r2, y_send, y_recv, coef,
    w_sem, t_sem, zs, zr, xs, xr, cs, cr, as_, ar, bs, br, ys, yr,
):
    X = T // 2
    spans, top, rows = ids.shape
    slots = table.shape[1]
    s = lax.axis_index("ep")
    j = lax.axis_index("tp")
    side = lax.rem(j, 2)
    xi = j // 2
    partner = xi * 2 + (1 - side)
    width = x.shape[3]
    parts = [pl.ds(c * rows, rows) for c in range(spans)]

    reads = [
        pltpu.make_async_copy(tokens.at[:, pl.ds(q * width, width)], x.at[0, q], t_sem.at[q])
        for q in range(T)
    ]
    loads = [pltpu.make_async_copy(weights.at[0, i], w.at[i], w_sem.at[i]) for i in range(3)]
    for copy in reads:
        copy.start()
    for copy in loads:
        copy.start()

    barrier = pltpu.get_barrier_semaphore()
    for k in range(1, E):
        pl.semaphore_signal(barrier, inc=1, device_id={"ep": lax.rem(s + k, E)}, device_id_type=MESH)
    for m in range(1, X):
        pl.semaphore_signal(
            barrier, inc=1, device_id={"tp": lax.rem(xi + m, X) * 2 + side}, device_id_type=MESH
        )
    pl.semaphore_signal(barrier, inc=1, device_id={"tp": partner}, device_id_type=MESH)
    for copy in reads:
        copy.wait()
    pl.semaphore_wait(barrier, E - 1 + X)

    def remote(src, dst, send, recv, where):
        return pltpu.make_async_remote_copy(
            src_ref=src, dst_ref=dst, send_sem=send, recv_sem=recv, device_id=where, device_id_type=MESH
        )

    def peer(m):
        return lax.rem(xi + m, X) * 2 + side

    def source(m):
        return lax.rem(xi - m + X, X) * 2 + side

    def z_copy(k, c):
        return remote(
            x.at[0, j, parts[c]], x.at[k, j, parts[c]], zs.at[k, c], zr.at[k, c],
            {"ep": lax.rem(s - k + E, E)},
        )

    def x_copy(k, m, c):
        piece = x.at[k, j, parts[c]]
        return remote(piece, piece, xs.at[k, m, c], xr.at[k, m, c], {"tp": peer(m)})

    def x_arrival(k, m, c):
        piece = x.at[k, source(m), parts[c]]
        return remote(piece, piece, xs.at[k, m, c], xr.at[k, m, c], {"tp": peer(m)})

    def core_copy(k, m, c):
        piece = x.at[k, source(m), parts[c]]
        return remote(piece, piece, cs.at[k, m, c], cr.at[k, m, c], {"tp": partner})

    def core_arrival(k, m, c):
        piece = x.at[k, lax.rem(xi - m + X, X) * 2 + (1 - side), parts[c]]
        return remote(piece, piece, cs.at[k, m, c], cr.at[k, m, c], {"tp": partner})

    def half_copy(k):
        return remote(p.at[k, 1 - side], r1.at[k], as_.at[k], ar.at[k], {"tp": partner})

    def sum_copy(k, m, c):
        there = lax.rem(xi + m, X)
        return remote(
            p.at[k, side, there, parts[c]], r2.at[k, m, parts[c]], bs.at[k, m, c], br.at[k, m, c],
            {"tp": peer(m)},
        )

    def y_copy(k, c):
        return remote(
            y_send.at[k, parts[c]], y_recv.at[k, parts[c]], ys.at[k, c], yr.at[k, c],
            {"ep": lax.rem(s + k, E)},
        )

    for k in range(1, E):
        for c in range(spans):
            z_copy(k, c).start()

    lane = lax.broadcasted_iota(jnp.int32, (1, slots), 1)
    earlier_rows = (
        lax.broadcasted_iota(jnp.int32, (rows, rows), 0) > lax.broadcasted_iota(jnp.int32, (rows, rows), 1)
    ).astype(jnp.float32).astype(jnp.bfloat16)
    limit = limits[...].astype(jnp.float32)

    def holders(c):
        held = jnp.zeros((1, slots), jnp.int32)
        order = jnp.zeros((1, slots), jnp.int32)
        for other in range(slots):
            same = (table[c : c + 1, :] == placement[c, other]).astype(jnp.int32)
            held = held + same
            order = order + jnp.where(lane > other, same, 0)
        return held, order

    lowest = holders(0)[1] == 0
    for c in range(spans):
        held, order = holders(c)
        picks = []
        ids_c, gates_c, replica_c = ids[c].T, gates[c].T, replica[c].T
        for member in range(top):
            chosen = ids_c[:, member : member + 1]
            remaining = jnp.broadcast_to(replica_c[:, member : member + 1], (rows, slots))
            for _ in range(3):
                remaining = jnp.where(remaining >= held, remaining - held, remaining)
            hit = jnp.logical_and(chosen == table[c : c + 1, :], remaining == order)
            picks.append(hit.astype(jnp.float32))
        before = jnp.dot(
            earlier_rows, functools.reduce(jnp.add, picks).astype(jnp.bfloat16),
            preferred_element_type=jnp.float32,
        )
        scale = jnp.zeros((rows, slots), jnp.float32)
        for member in range(top):
            kept = jnp.sum(jnp.where(before < limit, picks[member], 0.0), axis=1, keepdims=True)
            before = before + picks[member]
            serves = jnp.logical_and(ids_c[:, member : member + 1] == table[0:1, :], lowest)
            scale = scale + jnp.where(serves, kept * gates_c[:, member : member + 1], 0.0)
        for slot in range(slots):
            coef[slot, c * rows : (c + 1) * rows, :] = scale[:, slot : slot + 1]

    for copy in loads:
        copy.wait()

    def compute(k):
        def project(i):
            total = None
            for q in range(T):
                part = lax.dot_general(
                    w[i, :, q * width : (q + 1) * width], x[k, q],
                    (((1,), (1,)), ((), ())), preferred_element_type=jnp.float32,
                )
                total = part if total is None else total + part
            return total

        gate = project(0)
        upward = project(1)
        hidden = (gate / (1.0 + jnp.exp(-gate)) * upward).T.astype(jnp.bfloat16)
        for q in range(T):
            p[k, q % 2, q // 2] = jnp.dot(
                hidden, w[2, :, q * width : (q + 1) * width], preferred_element_type=jnp.float32
            ).astype(jnp.bfloat16)

    def finish(k):
        for c in range(spans):
            total = p[k, side, xi, parts[c]].astype(jnp.float32)
            for m in range(1, X):
                sum_copy(k, m, c).wait_recv()
                total = total + r2[k, m, parts[c]].astype(jnp.float32)
            y_send[k, parts[c]] = total.astype(jnp.bfloat16)

            @pl.when(k >= 1)
            def _():
                y_copy(k, c).start()

    def step(k, carry):
        compute(k)
        half_copy(k).start()

        @pl.when(k + 1 < E)
        def _():
            for c in range(spans):
                z_copy(k + 1, c).wait_recv()
                for m in range(1, X):
                    x_copy(k + 1, m, c).start()
                core_copy(k + 1, 0, c).start()

        half_copy(k).wait_recv()
        for c in range(spans):
            for m in range(X):
                p[k, side, m, parts[c]] = (
                    p[k, side, m, parts[c]].astype(jnp.float32) + r1[k, m, parts[c]].astype(jnp.float32)
                ).astype(jnp.bfloat16)
            for m in range(1, X):
                sum_copy(k, m, c).start()

        @pl.when(k >= 1)
        def _():
            finish(k - 1)

        @pl.when(k + 1 < E)
        def _():
            for c in range(spans):
                for m in range(1, X):
                    x_arrival(k + 1, m, c).wait_recv()
                    core_copy(k + 1, m, c).start()
            for c in range(spans):
                for m in range(X):
                    core_arrival(k + 1, m, c).wait_recv()

        return carry

    lax.fori_loop(0, E, step, 0)
    finish(E - 1)

    def weigh(rows, scale):
        return jnp.where(scale != 0, rows.astype(jnp.float32) * scale, 0.0)

    def combine(k, total):
        for c in range(spans):
            y_copy(k, c).wait_recv()
        return total + weigh(y_recv[k], coef[lax.rem(s - k + E, E)])

    total = lax.fori_loop(1, E, combine, weigh(y_send[0], coef[s]))
    out[...] = total.astype(jnp.bfloat16)

    def drain(k, carry):
        half_copy(k).wait_send()
        for c in range(spans):
            for m in range(1, X):
                sum_copy(k, m, c).wait_send()

        @pl.when(k >= 1)
        def _():
            for c in range(spans):
                z_copy(k, c).wait_send()
                for m in range(1, X):
                    x_copy(k, m, c).wait_send()
                for m in range(X):
                    core_copy(k, m, c).wait_send()
                y_copy(k, c).wait_send()

        return carry

    lax.fori_loop(0, E, drain, 0)


def held_plan(pattern):
    n = len(pattern)
    groups = [[s for s in range(n) if pattern[s] == e] for e in (0, 1)]
    host = [None] * n
    load = [0] * n
    order = sorted(range(n), key=lambda b: -len(groups[pattern[b]]))
    for b in order:
        others = groups[1 - pattern[b]]
        best = min(others, key=lambda h: (load[h], abs(h - b), -abs(2 * h - n + 1)))
        host[b] = best
        load[best] += 1
    served = [sorted((b for b in range(n) if host[b] == h), key=lambda b: abs(b - h)) for h in range(n)]
    return host, served


def routed_kernel(
    E, host, served, phases, halves,
    tokens, ids, gates, replica, table, limits, placement, weights, out,
    w, x, p, r1, r2, y, y_recv,
    w_sem, t_sem, zs, zr, xs, xr, cs, cr, as_, ar, bs, br, ys, yr,
):
    spans, top, rows = ids.shape
    slots = table.shape[1]
    M = spans * rows
    unit = M // phases
    s = lax.axis_index("ep")
    j = lax.axis_index("tp")
    side = lax.rem(j, 2)
    xi = j // 2

    def pick(values):
        total = 0
        for at, value in enumerate(values):
            total = total + jnp.where(s == at, value, 0)
        return total

    depth = max(len(blocks) for blocks in served)
    count = pick([len(blocks) for blocks in served])
    target = pick(host)
    place = pick([served[host[b]].index(b) for b in range(E)])

    def block_of(i):
        flat = 0
        for at, blocks in enumerate(served):
            for k, b in enumerate(blocks):
                flat = flat + jnp.where(jnp.logical_and(s == at, i == k), b, 0)
        return flat

    reads = [pltpu.make_async_copy(tokens, x.at[0], t_sem.at[0])]
    loads = [pltpu.make_async_copy(weights.at[0, i], w.at[i], w_sem.at[i]) for i in range(3)]
    for copy in reads:
        copy.start()
    for copy in loads:
        copy.start()

    edges = sorted({tuple(sorted((b, host[b]))) for b in range(E)})
    barrier = pltpu.get_barrier_semaphore()
    for a, b in edges:
        for me, other in ((a, b), (b, a)):
            @pl.when(s == me)
            def _():
                pl.semaphore_signal(barrier, inc=1, device_id={"ep": other}, device_id_type=MESH)
    core_peer = {"tp": xi * 2 + (1 - side)}
    x_peer = {"tp": (1 - xi) * 2 + side}
    pl.semaphore_signal(barrier, inc=1, device_id=core_peer, device_id_type=MESH)
    pl.semaphore_signal(barrier, inc=1, device_id=x_peer, device_id_type=MESH)

    def remote(src, dst, send, recv, where):
        return pltpu.make_async_remote_copy(
            src_ref=src, dst_ref=dst, send_sem=send, recv_sem=recv, device_id=where, device_id_type=MESH
        )

    quarter = unit // 4

    def piece(item, u, xh, core, half):
        if half:
            return x.at[item, pl.ds(pl.multiple_of(u * unit + (2 * xh + core) * quarter, quarter), quarter)]
        return x.at[item, pl.ds(pl.multiple_of(u * unit + core * 2 * quarter, 2 * quarter), 2 * quarter)]

    def token_send(ph, half):
        return remote(
            piece(0, ph, xi, side, half), piece(ph + 1, place, xi, side, half), zs.at[ph], zr.at[ph, place],
            {"ep": target},
        )

    def token_arrival(ph, i, half):
        here = piece(ph + 1, i, xi, side, half)
        return remote(here, here, zs.at[ph], zr.at[ph, i], {"ep": target})

    def across(ph, i):
        here = piece(ph + 1, i, xi, side, True)
        return remote(here, here, xs.at[ph, i], xr.at[ph, i], x_peer)

    def across_arrival(ph, i):
        here = piece(ph + 1, i, 1 - xi, side, True)
        return remote(here, here, xs.at[ph, i], xr.at[ph, i], x_peer)

    def beside(ph, i, t, half):
        here = piece(ph + 1, i, xi if t == 0 else 1 - xi, side, half)
        return remote(here, here, cs.at[ph, i, t], cr.at[ph, i, t], core_peer)

    def beside_arrival(ph, i, t, half):
        here = piece(ph + 1, i, xi if t == 0 else 1 - xi, 1 - side, half)
        return remote(here, here, cs.at[ph, i, t], cr.at[ph, i, t], core_peer)

    def half_copy(item, u):
        return remote(p.at[item, u, 1 - side], r1.at[item, u], as_.at[item, u], ar.at[item, u], core_peer)

    def sum_copy(item, u):
        return remote(p.at[item, u, side, 1 - xi], r2.at[item, u], bs.at[item, u], br.at[item, u], x_peer)

    def y_copy(ph, i):
        return remote(y.at[ph + 1, i], y_recv.at[ph], ys.at[ph, i], yr.at[ph], {"ep": block_of(i)})

    def y_arrival(ph):
        return remote(y.at[ph + 1, 0], y_recv.at[ph], ys.at[ph, 0], yr.at[ph], {"ep": target})

    def both(ph, action):
        if halves <= 0:
            action(False)
        elif halves >= phases:
            action(True)
        else:
            pl.when(ph < halves)(lambda: action(True))
            pl.when(ph >= halves)(lambda: action(False))

    lane = lax.broadcasted_iota(jnp.int32, (1, slots), 1)
    earlier_rows = (
        lax.broadcasted_iota(jnp.int32, (rows, rows), 0) > lax.broadcasted_iota(jnp.int32, (rows, rows), 1)
    ).astype(jnp.float32).astype(jnp.bfloat16)
    limit = limits[...].astype(jnp.float32)
    own_expert = placement[0, s]

    def holders(c):
        held = jnp.zeros((1, slots), jnp.int32)
        order = jnp.zeros((1, slots), jnp.int32)
        for other in range(slots):
            same = (table[c : c + 1, :] == placement[c, other]).astype(jnp.int32)
            held = held + same
            order = order + jnp.where(lane > other, same, 0)
        return held, order

    scales = []
    for c in range(spans):
        held, order = holders(c)
        picks = []
        ids_c, gates_c, replica_c = ids[c].T, gates[c].T, replica[c].T
        for member in range(top):
            chosen = ids_c[:, member : member + 1]
            remaining = jnp.broadcast_to(replica_c[:, member : member + 1], (rows, slots))
            for _ in range(3):
                remaining = jnp.where(remaining >= held, remaining - held, remaining)
            hit = jnp.logical_and(chosen == table[c : c + 1, :], remaining == order)
            picks.append(hit.astype(jnp.float32))
        before = jnp.dot(
            earlier_rows, functools.reduce(jnp.add, picks).astype(jnp.bfloat16),
            preferred_element_type=jnp.float32,
        )
        here = jnp.zeros((rows, 1), jnp.float32)
        there = jnp.zeros((rows, 1), jnp.float32)
        for member in range(top):
            kept = jnp.sum(jnp.where(before < limit, picks[member], 0.0), axis=1, keepdims=True)
            before = before + picks[member]
            scaled = kept * gates_c[:, member : member + 1]
            own = ids_c[:, member : member + 1] == own_expert
            here = here + jnp.where(own, scaled, 0.0)
            there = there + jnp.where(own, 0.0, scaled)
        scales.append((here, there))

    for copy in reads:
        copy.wait()
    pl.semaphore_wait(barrier, 2 + pick([sum(1 for e in edges if v in e) for v in range(E)]))

    for ph in range(phases):
        token_send(ph, ph < halves).start()

    for copy in loads:
        copy.wait()

    def units(item):
        return jnp.where(item == 0, phases, count)

    def gather(ph):
        def first(i, carry):
            def go(half):
                token_arrival(ph, i, half).wait_recv()
                if half:
                    across(ph, i).start()
                beside(ph, i, 0, half).start()
            both(ph, go)
            return carry

        def second(i, carry):
            def go(half):
                if half:
                    across_arrival(ph, i).wait_recv()
                    beside(ph, i, 1, half).start()
            both(ph, go)
            return carry

        def third(i, carry):
            def go(half):
                beside_arrival(ph, i, 0, half).wait_recv()
                if half:
                    beside_arrival(ph, i, 1, half).wait_recv()
            both(ph, go)
            return carry

        lax.fori_loop(0, count, first, 0)
        if halves > 0:
            lax.fori_loop(0, count, second, 0)
        lax.fori_loop(0, count, third, 0)

    width = y.shape[3]
    T = 4

    def compute(item):
        def project(i):
            return lax.dot_general(
                w[i], x[item], (((1,), (1,)), ((), ())), preferred_element_type=jnp.float32
            )

        gate = project(0)
        upward = project(1)
        hidden = (gate / (1.0 + jnp.exp(-gate)) * upward).T.astype(jnp.bfloat16)
        for q in range(T):
            part = jnp.dot(
                hidden, w[2, :, q * width : (q + 1) * width], preferred_element_type=jnp.float32
            ).astype(jnp.bfloat16)
            for u in range(phases):
                p[item, u, q % 2, q // 2] = part[u * unit : (u + 1) * unit]

    def reduce(item):
        def one(u, carry):
            half_copy(item, u).wait_recv()
            for m in range(2):
                p[item, u, side, m] = (
                    p[item, u, side, m].astype(jnp.float32) + r1[item, u, m].astype(jnp.float32)
                ).astype(jnp.bfloat16)
            sum_copy(item, u).start()
            return carry

        lax.fori_loop(0, units(item), one, 0)

    def finish(item):
        def one(u, carry):
            sum_copy(item, u).wait_recv()
            y[item, u] = (
                p[item, u, side, xi].astype(jnp.float32) + r2[item, u].astype(jnp.float32)
            ).astype(jnp.bfloat16)

            @pl.when(item >= 1)
            def _():
                y_copy(item - 1, u).start()

            return carry

        lax.fori_loop(0, units(item), one, 0)

    items = jnp.where(count > 0, phases + 1, 1)

    def step(item, carry):
        pl.when(item >= 1)(lambda: gather(item - 1))
        compute(item)

        def send(u, carry):
            half_copy(item, u).start()
            return carry

        lax.fori_loop(0, units(item), send, 0)
        pl.when(item >= 1)(lambda: finish(item - 1))
        reduce(item)
        return carry

    lax.fori_loop(0, items, step, 0)
    finish(items - 1)

    def weigh(values, scale):
        return jnp.where(scale != 0, values.astype(jnp.float32) * scale, 0.0)

    here = jnp.concatenate([scale[0] for scale in scales], axis=0)
    there = jnp.concatenate([scale[1] for scale in scales], axis=0)
    for ph in range(phases):
        y_arrival(ph).wait_recv()
        at = slice(ph * unit, (ph + 1) * unit)
        out[at] = (weigh(y[0, ph], here[at]) + weigh(y_recv[ph], there[at])).astype(jnp.bfloat16)

    for ph in range(phases):
        token_send(ph, ph < halves).wait_send()

    def drain(item, carry):
        def one(u, carry):
            half_copy(item, u).wait_send()
            sum_copy(item, u).wait_send()

            @pl.when(item >= 1)
            def _():
                ph = item - 1
                y_copy(ph, u).wait_send()

                def go(half):
                    beside(ph, u, 0, half).wait_send()
                    if half:
                        across(ph, u).wait_send()
                        beside(ph, u, 1, half).wait_send()
                both(ph, go)

            return carry

        return lax.fori_loop(0, units(item), one, carry)

    lax.fori_loop(0, items, drain, 0)


def routed(code, pattern, args, spans, rows, slots, E, hidden, model_width, width):
    host, served = held_plan(pattern)
    depth = max(len(blocks) for blocks in served)
    phases = 4 if depth > 1 else 2
    lone = [h for h in range(E) if len(served[h]) == depth]
    halves = 2 if depth > 1 and lone[0] in (0, E - 1) else 0
    halves = min(halves, phases)
    M = spans * rows
    unit = M // phases
    dma = pltpu.SemaphoreType.DMA
    any_, vmem, smem = (pl.BlockSpec(memory_space=space) for space in (pl.ANY, pltpu.VMEM, pltpu.SMEM))
    return pl.pallas_call(
        functools.partial(routed_kernel, E, host, served, phases, halves),
        out_shape=jax.ShapeDtypeStruct((M, width), jnp.bfloat16),
        in_specs=[any_, vmem, vmem, vmem, vmem, vmem, smem, any_],
        out_specs=vmem,
        scratch_shapes=[
            pltpu.VMEM((3, hidden, model_width), jnp.bfloat16),
            pltpu.VMEM((phases + 1, M, model_width), jnp.bfloat16),
            pltpu.VMEM((phases + 1, phases, 2, 2, unit, width), jnp.bfloat16),
            pltpu.VMEM((phases + 1, phases, 2, unit, width), jnp.bfloat16),
            pltpu.VMEM((phases + 1, phases, unit, width), jnp.bfloat16),
            pltpu.VMEM((phases + 1, phases, unit, width), jnp.bfloat16),
            pltpu.VMEM((phases, unit, width), jnp.bfloat16),
            dma((3,)), dma((1,)),
            dma((phases,)), dma((phases, depth)),
            dma((phases, depth)), dma((phases, depth)),
            dma((phases, depth, 2)), dma((phases, depth, 2)),
            dma((phases + 1, phases)), dma((phases + 1, phases)),
            dma((phases + 1, phases)), dma((phases + 1, phases)),
            dma((phases, depth)), dma((phases,)),
        ],
        compiler_params=pltpu.CompilerParams(
            collective_id=code, has_side_effects=True, vmem_limit_bytes=67043328
        ),
    )(*args)


def per_device(
    tokens, expert_ids, gate_weights, replica_pick, placement, slot_limit, expert_weights
):
    spans, rows, model_width = tokens.shape
    slots = placement.shape[1]
    E = lax.axis_size("ep")
    T = lax.axis_size("tp")
    X = T // 2
    width = model_width // T
    M = spans * rows
    hidden = expert_weights.shape[2]
    dma = pltpu.SemaphoreType.DMA
    args = (
        tokens.reshape(M, model_width), jnp.swapaxes(expert_ids, 1, 2), jnp.swapaxes(gate_weights, 1, 2),
        jnp.swapaxes(replica_pick, 1, 2), placement,
        slot_limit.reshape(1, slots), placement, expert_weights,
    )
    if expert_ids.shape[2] == 2 and slots == 4 and E == slots and X == 2:
        patterns = [tuple((0,) + tuple((m >> b) & 1 for b in range(slots - 1))) for m in range(1, 2 ** (slots - 1))]
        old = placement[0]
        weight = jnp.array([0] + [1 << b for b in range(slots - 1)], jnp.int32)
        which = jnp.sum(jnp.where(old != old[0], weight, 0)) - 1
        out = lax.switch(
            which,
            [
                functools.partial(
                    lambda code, pattern, *args: routed(
                        code, pattern, args, spans, rows, slots, E, hidden, model_width, width
                    ),
                    code, pattern,
                )
                for code, pattern in enumerate(patterns)
            ],
            *args,
        )
        return out.reshape(spans, rows, width)
    out = pl.pallas_call(
        functools.partial(kernel, E, T),
        out_shape=jax.ShapeDtypeStruct((M, width), jnp.bfloat16),
        in_specs=[
            pl.BlockSpec(memory_space=pl.ANY),
            pl.BlockSpec(memory_space=pltpu.VMEM),
            pl.BlockSpec(memory_space=pltpu.VMEM),
            pl.BlockSpec(memory_space=pltpu.VMEM),
            pl.BlockSpec(memory_space=pltpu.VMEM),
            pl.BlockSpec(memory_space=pltpu.VMEM),
            pl.BlockSpec(memory_space=pltpu.SMEM),
            pl.BlockSpec(memory_space=pl.ANY),
        ],
        out_specs=pl.BlockSpec(memory_space=pltpu.VMEM),
        scratch_shapes=[
            pltpu.VMEM((3, hidden, model_width), jnp.bfloat16),
            pltpu.VMEM((E, T, M, width), jnp.bfloat16),
            pltpu.VMEM((E, 2, X, M, width), jnp.bfloat16),
            pltpu.VMEM((E, X, M, width), jnp.bfloat16),
            pltpu.VMEM((E, X, M, width), jnp.bfloat16),
            pltpu.VMEM((E, M, width), jnp.bfloat16),
            pltpu.VMEM((E, M, width), jnp.bfloat16),
            pltpu.VMEM((slots, M, 1), jnp.float32),
            dma((3,)), dma((T,)),
            dma((E, spans)), dma((E, spans)),
            dma((E, X, spans)), dma((E, X, spans)),
            dma((E, X, spans)), dma((E, X, spans)),
            dma((E,)), dma((E,)),
            dma((E, X, spans)), dma((E, X, spans)),
            dma((E, spans)), dma((E, spans)),
        ],
        compiler_params=pltpu.CompilerParams(
            collective_id=0, has_side_effects=True, vmem_limit_bytes=67043328
        ),
    )(*args)
    return out.reshape(spans, rows, width)


def solution(mesh):
    placed = (
        P(None, ("groups", "ep"), None),
        P(None, ("groups", "ep"), None),
        P(None, ("groups", "ep"), None),
        P(None, ("groups", "ep"), None),
        P(),
        P(),
        P("ep", None, "tp", None),
    )
    return jax.shard_map(
        per_device,
        mesh=mesh,
        in_specs=placed,
        out_specs=P(None, ("groups", "ep"), "tp"),
        check_vma=False,
    )
```
